32 devices in a mesh: gx: 8 (over y, x, core), wa: 4 (over z).
Axes of the slice: x: 2, y: 2, z: 4, core: 2. Of those that a mesh axis runs over, the one named last changes fastest.
Arguments:
- feats: bfloat16 [8, 16, 8, 8, 8, 256], P('gx', 'wa'), may hold values from -6 to 6
- brick_ids: int32 [8, 16], P('gx', 'wa'), may hold values from 0 to 16, as said below
- conv3_w: bfloat16 [27, 256, 256], replicated, may hold values from -0.078125 to 0.078125
- conv3_scale: float32 [256], replicated, may hold values from 0.5 to 2
- conv3_bias: float32 [256], replicated, may hold values from -0.5 to 0.5
- bev_gain: float32 [256], replicated, may hold values from 0.5 to 2
- conv2_w: bfloat16 [9, 256, 256], replicated, may hold values from -0.125 to 0.125
- conv2_scale: float32 [256], replicated, may hold values from 0.5 to 2
- conv2_bias: float32 [256], replicated, may hold values from -0.5 to 0.5
Outputs:
- bev_out: bfloat16 [64, 128, 256], P('gx', 'wa')
The draws below stay inside these ranges and needn't reach their ends.
Inputs may be any that keep to these rules, and one draw needn't show every extreme that they name: `brick_ids`: for each g and each w < 4 / 2, slabs (g, w) and (g, w + 4 / 2) list exactly 4 occupied bricks together: slab w in its first k slots and slab w + 4 / 2 in its last 4 - k slots, with 1 <= k <= 3; the remaining slots hold 16; the bricks listed by one slab are distinct.
All inputs are finite; a program needn't handle non-finite values.
Results may differ from the reference program's by a relative error of at most 0.01.
Values may be sent and summed in bfloat16 or wider, within the bound.
A program may use at most 128 MiB of HBM per device.

```python
import math
import jax
import jax.numpy as jnp
from jax import lax

C = 256
BRICK = 8
BY = 16
SLOTS = 4
N_GX = 8
N_WA = 4


def shuffled_row(row_key):
    return jax.random.permutation(row_key, BY)


def draw_brick_ids(key, part):
    half_wa = N_WA // 2
    base_key = jax.random.fold_in(key, 11)
    count_key, order_key = jax.random.split(base_key)
    counts = jax.random.randint(count_key, (N_GX, half_wa), 1, SLOTS)
    counts = jnp.concatenate([counts, counts], axis=1)
    row_keys = jax.random.split(order_key, N_GX * N_WA)
    orders = jax.vmap(shuffled_row)(row_keys)
    chosen = orders[:, :SLOTS].reshape(N_GX, N_WA, SLOTS).astype(jnp.int32)
    slot_pos = jnp.arange(SLOTS, dtype=jnp.int32)[None, None, :]
    is_upper = (jnp.arange(N_WA) >= half_wa)[None, :, None]
    is_live = jnp.where(is_upper, slot_pos >= counts[:, :, None], slot_pos < counts[:, :, None])
    brick_list = jnp.where(is_live, chosen, BY)
    return brick_list.reshape(N_GX, N_WA * SLOTS).astype(jnp.int32)


def level_of(own_key, shape, cuts, least, high):
    gain = 1.0
    for axis_at, blocks in cuts:
        draws = jax.random.uniform(jax.random.fold_in(jax.random.fold_in(own_key, 6), axis_at), (blocks,), jnp.float32, least / len(cuts), high / len(cuts))
        gain = gain * jnp.repeat(jnp.exp(draws), shape[axis_at] // blocks).reshape((-1,) + (1,) * (len(shape) - 1 - axis_at))
    return gain


def bell_draw(rng, dims, deviation, reach, shards=(), kind=jnp.bfloat16):
    values = deviation * jax.random.normal(rng, dims, jnp.float32)
    if shards:
        values = values * level_of(rng, dims, shards, -0.22, 0.18)
    return jnp.clip(values, -reach, reach).astype(kind)


def setup_inputs(seed: int = 0) -> dict:
    keys = jax.random.split(jax.random.key(seed), 10)
    feats = bell_draw(keys[0], (N_GX, N_WA * SLOTS, BRICK, BRICK, BRICK, C), 1.0, 6.0, ((0, 8), (1, 4)))
    brick_ids = draw_brick_ids(jax.random.fold_in(keys[9], 71), 0)
    conv3_w = bell_draw(keys[2], (27, C, C), (27 * C) ** -0.5, 0.078125)
    conv3_scale = jnp.clip(jnp.exp(jax.random.uniform(keys[3], (C,), jnp.float32, math.log(0.5), math.log(2.0))), 0.5, 2.0)
    conv3_bias = jnp.clip(jax.random.uniform(keys[4], (C,), jnp.float32, -0.5, 0.5), -0.5, 0.5)
    bev_gain = jnp.clip(jnp.exp(jax.random.uniform(keys[5], (C,), jnp.float32, math.log(0.5), math.log(2.0))), 0.5, 2.0)
    conv2_w = bell_draw(keys[6], (9, C, C), (9 * C) ** -0.5, 0.125)
    conv2_scale = jnp.clip(jnp.exp(jax.random.uniform(keys[7], (C,), jnp.float32, math.log(0.5), math.log(2.0))), 0.5, 2.0)
    conv2_bias = jnp.clip(jax.random.uniform(keys[8], (C,), jnp.float32, -0.5, 0.5), -0.5, 0.5)
    return {"feats": feats, "brick_ids": brick_ids, "conv3_w": conv3_w, "conv3_scale": conv3_scale, "conv3_bias": conv3_bias, "bev_gain": bev_gain, "conv2_w": conv2_w, "conv2_scale": conv2_scale, "conv2_bias": conv2_bias}


def conv_volume(padded_tiles, weights, brick_edge):
    channels = padded_tiles.shape[-1]
    summed = jnp.zeros((padded_tiles.shape[0] * brick_edge ** 3, channels), jnp.float32)
    for offset in range(27):
        shift_x, shift_y, shift_z = (offset // 9, offset // 3 % 3, offset % 3)
        window = padded_tiles[:, shift_x:shift_x + brick_edge, shift_y:shift_y + brick_edge, shift_z:shift_z + brick_edge]
        summed = summed + jnp.dot(window.reshape(-1, channels), weights[offset], preferred_element_type=jnp.float32)
    return summed.reshape(padded_tiles.shape[0], brick_edge, brick_edge, brick_edge, channels)

def brick_block(padded_tiles, weights, conv_scale, conv_bias, brick_edge):
    conv_out = conv_volume(padded_tiles, weights, brick_edge)
    center = padded_tiles[:, 1:brick_edge + 1, 1:brick_edge + 1, 1:brick_edge + 1].astype(jnp.float32)
    return jax.nn.relu(conv_out * conv_scale + conv_bias + center).astype(jnp.bfloat16)

def rms_norm(plane, gain_vec):
    mean_sq = lax.optimization_barrier(jnp.mean(plane * plane, axis=-1, keepdims=True))
    return (plane / jnp.sqrt(mean_sq + 1e-05) * gain_vec).astype(jnp.bfloat16)

def plane_block(normed_pad, weights, conv_scale, conv_bias, residual):
    rows_x, rows_y, channels = residual.shape
    summed = jnp.zeros((rows_x * rows_y, channels), jnp.float32)
    for offset in range(9):
        shift_x, shift_y = (offset // 3, offset % 3)
        window = normed_pad[shift_x:shift_x + rows_x, shift_y:shift_y + rows_y].reshape(-1, channels)
        summed = summed + jnp.dot(window, weights[offset], preferred_element_type=jnp.float32)
    summed = summed.reshape(rows_x, rows_y, channels)
    return (jax.nn.relu(summed * conv_scale + conv_bias) + residual.astype(jnp.float32)).astype(jnp.bfloat16)

def reference(feats, brick_ids, conv3_w, conv3_scale, conv3_bias, bev_gain, conv2_w, conv2_scale, conv2_bias):
    brick_edge = feats.shape[2]
    channels = feats.shape[-1]
    half_wa = N_WA // 2
    listed = brick_ids.reshape(N_GX, N_WA, SLOTS)
    tiles = feats.reshape(N_GX, N_WA, SLOTS, brick_edge, brick_edge, brick_edge, channels)
    holder = jnp.zeros((N_GX, N_WA, BY + 1, brick_edge, brick_edge, brick_edge, channels), jnp.bfloat16)
    gx_index = jnp.arange(N_GX, dtype=jnp.int32)[:, None, None]
    wa_index = jnp.arange(N_WA, dtype=jnp.int32)[None, :, None]
    holder = holder.at[gx_index, wa_index, listed].set(tiles)
    scene = holder[:, :, :BY].transpose(0, 3, 2, 4, 1, 5, 6)
    scene = scene.reshape(N_GX * brick_edge, BY * brick_edge, N_WA * brick_edge, channels)
    padded = jnp.pad(scene, ((1, 1), (1, 1), (1, 1), (0, 0)))
    low_list = listed[:, :half_wa]
    high_list = listed[:, half_wa:]
    low_live = low_list < BY
    merged = jnp.where(low_live, low_list, high_list).astype(jnp.int32)
    slab_z = jnp.where(low_live, wa_index[:, :half_wa], wa_index[:, :half_wa] + half_wa).astype(jnp.int32)
    slab_x = jnp.broadcast_to(gx_index, merged.shape).astype(jnp.int32)
    visits = (slab_x.reshape(-1), merged.reshape(-1), slab_z.reshape(-1))

    def visit(plane, item):
        pos_x, pos_y, pos_z = item
        zero_index = jnp.zeros((), jnp.int32)
        start_x = (pos_x * brick_edge).astype(jnp.int32)
        start_y = (pos_y * brick_edge).astype(jnp.int32)
        start_z = (pos_z * brick_edge).astype(jnp.int32)
        box_size = brick_edge + 2
        region = lax.dynamic_slice(padded, (start_x, start_y, start_z, zero_index), (box_size, box_size, box_size, channels))
        block = brick_block(region[None], conv3_w, conv3_scale, conv3_bias, brick_edge)[0]
        column = lax.optimization_barrier(jnp.sum(block.astype(jnp.float32), axis=2))
        current = lax.dynamic_slice(plane, (start_x, start_y, zero_index), (brick_edge, brick_edge, channels))
        plane = lax.dynamic_update_slice(plane, current + column, (start_x, start_y, zero_index))
        return (plane, None)
    plane_init = jnp.zeros((N_GX * brick_edge, BY * brick_edge, channels), jnp.float32)
    plane, unused = lax.scan(visit, plane_init, visits)
    normed = rms_norm(plane, bev_gain)
    normed_pad = jnp.pad(normed, ((1, 1), (1, 1), (0, 0)))
    return plane_block(normed_pad, conv2_w, conv2_scale, conv2_bias, normed)
```

```python
import functools

import jax
import jax.numpy as jnp
from jax import lax
from jax.experimental import pallas as pl
from jax.experimental.pallas import tpu as pltpu
from jax.sharding import PartitionSpec as P

BY = 16
GONE = -99
FAR = -1000
MESH = pl.DeviceIdType.MESH
F32 = jnp.float32
BF16 = jnp.bfloat16


def side(sign):
    return 0 if sign < 0 else 1


def block_kernel(
    ng, nw, live,
    ids_ref, feats_ref, w3_ref, w2_ref, scale3_ref, bias3_ref, gain_ref, scale2_ref, bias2_ref,
    out_ref,
    tiles, vol, zsend, zrecv, xrecv, erecv, idsend, idrecv, zpad, cols_lhs, w3, w2,
    csend, crecv, xedge, plane, lhs2,
    load_sem, id_s, id_r, x_s, x_r, z_s, z_r, e_s, e_r, c_s, c_r,
):
    g = lax.axis_index("gx")
    w = lax.axis_index("wa")
    edge = tiles.shape[1]
    chans = tiles.shape[-1]
    ydev = out_ref.shape[1]
    per_slab = ydev // edge
    first = jnp.where(w < nw // 2, 0, feats_ref.shape[1] - live)

    def has_x(d):
        return jnp.logical_and(g + d >= 0, g + d < ng)

    def has_z(e):
        return jnp.logical_and(w + e >= 0, w + e < nw)

    def present(d, peer):
        return has_x(d) if d else w != peer

    peers = [(d, peer) for d in (0, -1, 1) for peer in range(nw)]

    load = pltpu.make_async_copy(feats_ref.at[0, pl.ds(first, live)], tiles, load_sem.at[0])
    load.start()
    load_w3 = pltpu.make_async_copy(w3_ref, w3, load_sem.at[1])
    load_w3.start()
    load_w2 = pltpu.make_async_copy(w2_ref, w2, load_sem.at[2])
    load_w2.start()

    barrier = pltpu.get_barrier_semaphore()
    for d, peer in peers:
        @pl.when(present(d, peer))
        def _():
            pl.semaphore_signal(barrier, inc=1, device_id=(g + d, peer), device_id_type=MESH)

    own = [ids_ref[0, first + j] for j in range(live)]
    row = lax.broadcasted_iota(jnp.int32, idsend.shape, 0)
    listed = jnp.full(idsend.shape, GONE, jnp.int32)
    for j in range(live):
        listed = jnp.where(row == j, jnp.where(own[j] < BY, own[j], GONE), listed)
    idsend[...] = listed
    idrecv[1, w] = listed
    for d in (-1, 1):
        @pl.when(jnp.logical_not(has_x(d)))
        def _():
            for peer in range(nw):
                idrecv[1 + d, peer] = jnp.full(idsend.shape, GONE, jnp.int32)

    load.wait()
    for s in range(live):
        vol[s, 1 : edge + 1, edge : edge * (edge + 1), :] = (
            tiles[s].astype(F32).reshape(edge, edge * edge, chans)
        )
    for s in range(live):
        for e, z in ((-1, 0), (1, edge - 1)):
            zsend[side(e), s] = tiles[s].astype(F32)[:, :, z, :].astype(BF16)

    count = (1 + has_x(-1).astype(jnp.int32) + has_x(1).astype(jnp.int32)) * nw - 1
    pl.semaphore_wait(barrier, count)

    def id_copy(d, peer):
        return pltpu.make_async_remote_copy(
            src_ref=idsend, dst_ref=idrecv.at[1 - d, w],
            send_sem=id_s.at[1 + d, peer], recv_sem=id_r.at[1 - d, w],
            device_id=(g + d, peer), device_id_type=MESH,
        )

    def id_arrival(d, peer):
        return pltpu.make_async_remote_copy(
            src_ref=idsend, dst_ref=idrecv.at[1 + d, peer],
            send_sem=id_s.at[1 + d, peer], recv_sem=id_r.at[1 + d, peer],
            device_id=(g + d, peer), device_id_type=MESH,
        )

    def x_copy(d, arrival=False):
        to = side(d) if arrival else side(-d)
        return pltpu.make_async_remote_copy(
            src_ref=tiles.at[:, 0 if d < 0 else edge - 1], dst_ref=xrecv.at[to],
            send_sem=x_s.at[side(d)], recv_sem=x_r.at[to],
            device_id=(g + d, w), device_id_type=MESH,
        )

    def z_copy(e, arrival=False):
        to = side(e) if arrival else side(-e)
        return pltpu.make_async_remote_copy(
            src_ref=zsend.at[side(e)], dst_ref=zrecv.at[to],
            send_sem=z_s.at[side(e)], recv_sem=z_r.at[to],
            device_id=(g, w + e), device_id_type=MESH,
        )

    def e_copy(d, e, arrival=False):
        tx, tz = (side(d), side(e)) if arrival else (side(-d), side(-e))
        return pltpu.make_async_remote_copy(
            src_ref=zsend.at[side(e), :, 0 if d < 0 else edge - 1], dst_ref=erecv.at[tx, tz],
            send_sem=e_s.at[side(d), side(e)], recv_sem=e_r.at[tx, tz],
            device_id=(g + d, w + e), device_id_type=MESH,
        )

    for d in (-1, 1):
        @pl.when(has_x(d))
        def _():
            x_copy(d).start()
    for e in (-1, 1):
        @pl.when(has_z(e))
        def _():
            z_copy(e).start()
    for d in (-1, 1):
        for e in (-1, 1):
            @pl.when(jnp.logical_and(has_x(d), has_z(e)))
            def _():
                e_copy(d, e).start()
    for d, peer in peers:
        @pl.when(present(d, peer))
        def _():
            id_copy(d, peer).start()

    def picked(ids, target, shape, value):
        total = jnp.zeros(shape, F32)
        for j in range(live):
            hit = jnp.broadcast_to(ids[j : j + 1].reshape((1,) * (len(shape) - 1) + (chans,)), shape)
            total = jnp.where(hit == target, value(j), total)
        return total

    last = edge * edge
    for s in range(live):
        vol[s, 1 : edge + 1, 0:edge, :] = picked(
            listed, own[s] - 1, (edge, edge, chans), lambda j: vol[j, 1 : edge + 1, last : last + edge, :]
        )
        vol[s, 1 : edge + 1, last + edge : last + 2 * edge, :] = picked(
            listed, own[s] + 1, (edge, edge, chans), lambda j: vol[j, 1 : edge + 1, edge : 2 * edge, :]
        )

    for d, peer in peers:
        @pl.when(present(d, peer))
        def _():
            id_copy(d, peer).wait_send()
            id_arrival(d, peer).wait_recv()
    for d in (-1, 1):
        @pl.when(has_x(d))
        def _():
            x_copy(d).wait_send()
            x_copy(d, True).wait_recv()

    for d in (-1, 1):
        ids = idrecv[1 + d, w]
        px = 0 if d < 0 else edge + 1
        for s in range(live):
            vol[s, px, edge : last + edge, :] = picked(
                ids, own[s], (edge, edge, chans), lambda j: xrecv[side(d), j].astype(F32)
            ).reshape(last, chans)
            vol[s, px, 0:edge, :] = picked(
                ids, own[s] - 1, (edge, chans), lambda j: xrecv[side(d), j, edge - 1].astype(F32)
            )
            vol[s, px, last + edge : last + 2 * edge, :] = picked(
                ids, own[s] + 1, (edge, chans), lambda j: xrecv[side(d), j, 0].astype(F32)
            )

    for e in (-1, 1):
        @pl.when(has_z(e))
        def _():
            z_copy(e).wait_send()
            z_copy(e, True).wait_recv()
    for d in (-1, 1):
        for e in (-1, 1):
            @pl.when(jnp.logical_and(has_x(d), has_z(e)))
            def _():
                e_copy(d, e).wait_send()
                e_copy(d, e, True).wait_recv()

    for e in (-1, 1):
        at = jnp.clip(w + e, 0, nw - 1)
        for s in range(live):
            target = jnp.where(has_z(e), own[s], FAR)
            for d in (0, -1, 1):
                ids = idrecv[1 + d, at]
                if d == 0:
                    where_x = slice(1, edge + 1)
                    shape = (edge, edge, chans)
                    value = lambda j: zrecv[side(e), j].astype(F32)
                else:
                    where_x = slice(0, 1) if d < 0 else slice(edge + 1, edge + 2)
                    shape = (1, edge, chans)
                    value = lambda j: erecv[side(d), side(e), j].astype(F32)[None]
                zpad[s, side(e), where_x, 1 : edge + 1, :] = picked(ids, target, shape, value)
                zpad[s, side(e), where_x, 0:1, :] = picked(ids, target - 1, shape, value)[
                    :, edge - 1 : edge
                ]
                zpad[s, side(e), where_x, edge + 1 : edge + 2, :] = picked(
                    ids, target + 1, shape, value
                )[:, 0:1]

    pad = edge + 2
    half = edge // 2
    reach = half + 2
    zrow = lax.broadcasted_iota(jnp.int32, (pad, edge, chans), 1)

    def build(step, carry):
        s = step // reach
        xl = step % reach
        low, mid, high = [], [], []
        for xh in range(2):
            px = xl + half * xh
            v = vol[s, px].reshape(pad, edge, chans)
            below = jnp.broadcast_to(zpad[s, 0, px, 0:pad, :][:, None, :], (pad, edge, chans))
            above = jnp.broadcast_to(zpad[s, 1, px, 0:pad, :][:, None, :], (pad, edge, chans))
            low.append(jnp.where(zrow == 0, below, pltpu.roll(v, 1, axis=1)))
            mid.append(v)
            high.append(jnp.where(zrow == edge - 1, above, pltpu.roll(v, edge - 1, axis=1)))
        for c, pair in enumerate((low, mid, high)):
            cols_lhs[s, xl, :, :, c * chans : (c + 1) * chans] = jnp.concatenate(
                pair, axis=1
            ).astype(BF16)
        return carry

    lax.fori_loop(0, live * reach, build, 0)

    load_w3.wait()
    rows = edge * edge * edge
    out_row = lax.broadcasted_iota(jnp.int32, (last, rows), 0)
    in_row = lax.broadcasted_iota(jnp.int32, (last, rows), 1)
    in_pair = in_row // edge
    in_y = (in_pair // 2) % edge
    in_x = in_pair // (2 * edge) + half * (in_pair % 2)
    pool = jnp.where(in_x * edge + in_y == out_row, 1.0, 0.0).astype(BF16)

    def conv(s, carry):
        acc = jnp.zeros((rows, chans), F32)
        for a in range(3):
            for b in range(3):
                window = cols_lhs[s, pl.ds(a, half), pl.ds(b, edge)].reshape(rows, 3 * chans)
                acc = acc + jnp.dot(window, w3[3 * a + b], preferred_element_type=F32)
        center = cols_lhs[s, pl.ds(1, half), pl.ds(1, edge), :, chans : 2 * chans]
        block = acc * scale3_ref[...] + bias3_ref[...] + center.reshape(rows, chans).astype(F32)
        block = jnp.maximum(block, 0.0).astype(BF16)
        summed = jnp.dot(pool, block, preferred_element_type=F32)
        live_row = ids_ref[0, first + s]
        keep = jnp.full((last, chans), live_row, jnp.int32) < BY
        summed = jnp.where(keep, summed, 0.0).reshape(edge, edge, chans).astype(BF16)
        csend[s] = summed
        crecv[w, s] = summed
        return carry

    lax.fori_loop(0, live, conv, 0)

    def c_copy(d, peer, arrival=False):
        src = csend if d == 0 else csend.at[:, 0 if d < 0 else edge - 1]
        if arrival:
            dst = crecv.at[peer] if d == 0 else xedge.at[side(d), peer]
            sem = c_r.at[1 + d, peer]
        else:
            dst = crecv.at[w] if d == 0 else xedge.at[side(-d), w]
            sem = c_r.at[1 - d, w]
        return pltpu.make_async_remote_copy(
            src_ref=src, dst_ref=dst, send_sem=c_s.at[1 + d, peer], recv_sem=sem,
            device_id=(g + d, peer), device_id_type=MESH,
        )

    for d, peer in peers:
        @pl.when(present(d, peer))
        def _():
            c_copy(d, peer).start()
    load_w2.wait()
    for d, peer in peers:
        @pl.when(present(d, peer))
        def _():
            c_copy(d, peer).wait_send()
            c_copy(d, peer, True).wait_recv()

    off = edge
    for d in (0, -1, 1):
        where_x = slice(1, edge + 1) if d == 0 else (slice(0, 1) if d < 0 else slice(edge + 1, edge + 2))
        shape = (edge if d == 0 else 1, edge, chans)
        for q in range(-1, per_slab + 1):
            total = jnp.zeros(shape, F32)
            for peer in range(nw):
                ids = idrecv[1 + d, peer]
                for j in range(live):
                    hit = jnp.broadcast_to(ids[j : j + 1].reshape(1, 1, chans), shape)
                    if d == 0:
                        value = crecv[peer, j].astype(F32)
                    else:
                        value = xedge[side(d), peer, j].astype(F32)[None]
                    total = total + jnp.where(hit == w * per_slab + q, value, 0.0)
            scale = lax.rsqrt(jnp.mean(total * total, axis=-1, keepdims=True) + 1e-05)
            normed = total * scale * gain_ref[...].reshape(1, 1, chans)
            begin = off + q * edge
            plane[where_x, begin : begin + edge, :] = normed

    for c in range(3):
        lhs2[:, :, c * chans : (c + 1) * chans] = plane[
            :, off + c - 1 : off + c - 1 + ydev, :
        ].astype(BF16)
    total = jnp.zeros((edge * ydev, chans), F32)
    for a in range(3):
        total = total + jnp.dot(
            lhs2[a : a + edge].reshape(edge * ydev, 3 * chans), w2[a], preferred_element_type=F32
        )
    residual = lhs2[1 : edge + 1, :, chans : 2 * chans].reshape(edge * ydev, chans).astype(F32)
    result = jnp.maximum(total * scale2_ref[...] + bias2_ref[...], 0.0) + residual
    out_ref[...] = result.reshape(edge, ydev, chans).astype(BF16)


def per_device(
    ng, nw,
    feats, brick_ids, conv3_w, conv3_scale, conv3_bias, bev_gain, conv2_w, conv2_scale, conv2_bias,
):
    slots, edge, chans = feats.shape[1], feats.shape[2], feats.shape[-1]
    live = slots - 1
    ydev = BY * edge // nw
    pad = edge + 2
    reach = edge // 2 + 2
    vmem = pl.BlockSpec(memory_space=pltpu.VMEM)
    hbm = pl.BlockSpec(memory_space=pl.ANY)
    dma = pltpu.SemaphoreType.DMA
    return pl.pallas_call(
        functools.partial(block_kernel, ng, nw, live),
        out_shape=jax.ShapeDtypeStruct((edge, ydev, chans), BF16),
        in_specs=[pl.BlockSpec(memory_space=pltpu.SMEM), hbm, hbm, hbm] + [vmem] * 5,
        out_specs=vmem,
        scratch_shapes=[
            pltpu.VMEM((live, edge, edge, edge, chans), BF16),
            pltpu.VMEM((live, pad, pad * edge, chans), F32),
            pltpu.VMEM((2, live, edge, edge, chans), BF16),
            pltpu.VMEM((2, live, edge, edge, chans), BF16),
            pltpu.VMEM((2, live, edge, edge, chans), BF16),
            pltpu.VMEM((2, 2, live, edge, chans), BF16),
            pltpu.VMEM((8, chans), jnp.int32),
            pltpu.VMEM((3, nw, 8, chans), jnp.int32),
            pltpu.VMEM((live, 2, pad, 16, chans), F32),
            pltpu.VMEM((live, reach, pad, 2 * edge, 3 * chans), BF16),
            pltpu.VMEM((9, 3 * chans, chans), BF16),
            pltpu.VMEM((3, 3 * chans, chans), BF16),
            pltpu.VMEM((live, edge, edge, chans), BF16),
            pltpu.VMEM((nw, live, edge, edge, chans), BF16),
            pltpu.VMEM((2, nw, live, edge, chans), BF16),
            pltpu.VMEM((pad, ydev + 2 * edge, chans), F32),
            pltpu.VMEM((pad, ydev, 3 * chans), BF16),
            dma((3,)),
            dma((3, nw)), dma((3, nw)),
            dma((2,)), dma((2,)),
            dma((2,)), dma((2,)),
            dma((2, 2)), dma((2, 2)),
            dma((3, nw)), dma((3, nw)),
        ],
        compiler_params=pltpu.CompilerParams(
            collective_id=0, has_side_effects=True, vmem_limit_bytes=56 << 20
        ),
    )(
        brick_ids,
        feats,
        conv3_w.reshape(9, 3 * chans, chans),
        conv2_w.reshape(3, 3 * chans, chans),
        conv3_scale.reshape(1, chans),
        conv3_bias.reshape(1, chans),
        bev_gain.reshape(1, chans),
        conv2_scale.reshape(1, chans),
        conv2_bias.reshape(1, chans),
    )


def solution(mesh):
    return jax.shard_map(
        functools.partial(per_device, mesh.shape["gx"], mesh.shape["wa"]),
        mesh=mesh,
        in_specs=(
            P("gx", "wa", None, None, None, None),
            P("gx", "wa"),
            P(),
            P(),
            P(),
            P(),
            P(),
            P(),
            P(),
        ),
        out_specs=P("gx", "wa", None),
        check_vma=False,
    )
```

```python
import functools

import jax
import jax.numpy as jnp
from jax import lax
from jax.experimental import pallas as pl
from jax.experimental.pallas import tpu as pltpu
from jax.sharding import PartitionSpec as P

BY = 16
GONE = -99
FAR = -1000
MESH = pl.DeviceIdType.MESH
F32 = jnp.float32
BF16 = jnp.bfloat16


def side(sign):
    return 0 if sign < 0 else 1


def block_kernel(
    ng, nw, live,
    ids_ref, feats_ref, w3_ref, w2_ref, scale3_ref, bias3_ref, gain_ref, scale2_ref, bias2_ref,
    out_ref,
    tiles, vol, zsend, zrecv, xrecv, erecv, idsend, idrecv, zpad, cols_lhs, w3, w2,
    csend, crecv, xedge, plane, lhs2,
    load_sem, id_s, id_r, x_s, x_r, z_s, z_r, e_s, e_r, c_s, c_r,
):
    g = lax.axis_index("gx")
    w = lax.axis_index("wa")
    edge = tiles.shape[1]
    chans = tiles.shape[-1]
    ydev = out_ref.shape[1]
    per_slab = ydev // edge
    first = jnp.where(w < nw // 2, 0, feats_ref.shape[1] - live)

    def has_x(d):
        return jnp.logical_and(g + d >= 0, g + d < ng)

    def has_z(e):
        return jnp.logical_and(w + e >= 0, w + e < nw)

    def present(d, peer):
        return has_x(d) if d else w != peer

    peers = [(d, peer) for d in (0, -1, 1) for peer in range(nw)]

    def near(d, peer):
        return jnp.logical_and(present(d, peer), jnp.abs(w - peer) <= 1)

    def far(d, peer):
        return jnp.logical_and(present(d, peer), jnp.abs(w - peer) > 1)

    load = pltpu.make_async_copy(feats_ref.at[0, pl.ds(first, live)], tiles, load_sem.at[0])
    load.start()
    load_w3 = pltpu.make_async_copy(w3_ref, w3, load_sem.at[1])
    load_w3.start()
    load_w2 = pltpu.make_async_copy(w2_ref, w2, load_sem.at[2])
    load_w2.start()

    barrier = pltpu.get_barrier_semaphore()
    for d, peer in peers:
        @pl.when(present(d, peer))
        def _():
            pl.semaphore_signal(barrier, inc=1, device_id=(g + d, peer), device_id_type=MESH)

    own = [ids_ref[0, first + j] for j in range(live)]
    row = lax.broadcasted_iota(jnp.int32, idsend.shape, 0)
    listed = jnp.full(idsend.shape, GONE, jnp.int32)
    for j in range(live):
        listed = jnp.where(row == j, jnp.where(own[j] < BY, own[j], GONE), listed)
    idsend[...] = listed
    idrecv[1, w] = listed
    for d in (-1, 1):
        @pl.when(jnp.logical_not(has_x(d)))
        def _():
            for peer in range(nw):
                idrecv[1 + d, peer] = jnp.full(idsend.shape, GONE, jnp.int32)

    load.wait()
    for s in range(live):
        vol[s, 1 : edge + 1, edge : edge * (edge + 1), :] = (
            tiles[s].astype(F32).reshape(edge, edge * edge, chans)
        )
    for s in range(live):
        for e, z in ((-1, 0), (1, edge - 1)):
            zsend[side(e), s] = tiles[s].astype(F32)[:, :, z, :].astype(BF16)

    count = (1 + has_x(-1).astype(jnp.int32) + has_x(1).astype(jnp.int32)) * nw - 1
    pl.semaphore_wait(barrier, count)

    def id_copy(d, peer):
        return pltpu.make_async_remote_copy(
            src_ref=idsend, dst_ref=idrecv.at[1 - d, w],
            send_sem=id_s.at[1 + d, peer], recv_sem=id_r.at[1 - d, w],
            device_id=(g + d, peer), device_id_type=MESH,
        )

    def id_arrival(d, peer):
        return pltpu.make_async_remote_copy(
            src_ref=idsend, dst_ref=idrecv.at[1 + d, peer],
            send_sem=id_s.at[1 + d, peer], recv_sem=id_r.at[1 + d, peer],
            device_id=(g + d, peer), device_id_type=MESH,
        )

    def x_copy(d, arrival=False):
        to = side(d) if arrival else side(-d)
        return pltpu.make_async_remote_copy(
            src_ref=tiles.at[:, 0 if d < 0 else edge - 1], dst_ref=xrecv.at[to],
            send_sem=x_s.at[side(d)], recv_sem=x_r.at[to],
            device_id=(g + d, w), device_id_type=MESH,
        )

    def z_copy(e, arrival=False):
        to = side(e) if arrival else side(-e)
        return pltpu.make_async_remote_copy(
            src_ref=zsend.at[side(e)], dst_ref=zrecv.at[to],
            send_sem=z_s.at[side(e)], recv_sem=z_r.at[to],
            device_id=(g, w + e), device_id_type=MESH,
        )

    def e_copy(d, e, arrival=False):
        tx, tz = (side(d), side(e)) if arrival else (side(-d), side(-e))
        return pltpu.make_async_remote_copy(
            src_ref=zsend.at[side(e), :, 0 if d < 0 else edge - 1], dst_ref=erecv.at[tx, tz],
            send_sem=e_s.at[side(d), side(e)], recv_sem=e_r.at[tx, tz],
            device_id=(g + d, w + e), device_id_type=MESH,
        )

    for e in (-1, 1):
        @pl.when(has_z(e))
        def _():
            z_copy(e).start()
    for d in (-1, 1):
        @pl.when(has_x(d))
        def _():
            x_copy(d).start()
    for d in (-1, 1):
        for e in (-1, 1):
            @pl.when(jnp.logical_and(has_x(d), has_z(e)))
            def _():
                e_copy(d, e).start()
    for d, peer in peers:
        @pl.when(near(d, peer))
        def _():
            id_copy(d, peer).start()

    def picked(ids, target, shape, value):
        total = jnp.zeros(shape, F32)
        for j in range(live):
            wide = jnp.concatenate([ids[j : j + 1]] * 2, axis=1)
            hit = jnp.broadcast_to(wide.reshape((1,) * (len(shape) - 1) + (chans,)), shape)
            total = jnp.where(hit == target, value(j), total)
        return total

    last = edge * edge
    for s in range(live):
        vol[s, 1 : edge + 1, 0:edge, :] = picked(
            listed, own[s] - 1, (edge, edge, chans), lambda j: vol[j, 1 : edge + 1, last : last + edge, :]
        )
        vol[s, 1 : edge + 1, last + edge : last + 2 * edge, :] = picked(
            listed, own[s] + 1, (edge, edge, chans), lambda j: vol[j, 1 : edge + 1, edge : 2 * edge, :]
        )

    for d, peer in peers:
        @pl.when(near(d, peer))
        def _():
            id_copy(d, peer).wait_send()
            id_arrival(d, peer).wait_recv()
    for d in (-1, 1):
        @pl.when(has_x(d))
        def _():
            x_copy(d).wait_send()
            x_copy(d, True).wait_recv()

    for d in (-1, 1):
        ids = idrecv[1 + d, w]
        px = 0 if d < 0 else edge + 1
        for s in range(live):
            vol[s, px, edge : last + edge, :] = picked(
                ids, own[s], (edge, edge, chans), lambda j: xrecv[side(d), j].astype(F32)
            ).reshape(last, chans)
            vol[s, px, 0:edge, :] = picked(
                ids, own[s] - 1, (edge, chans), lambda j: xrecv[side(d), j, edge - 1].astype(F32)
            )
            vol[s, px, last + edge : last + 2 * edge, :] = picked(
                ids, own[s] + 1, (edge, chans), lambda j: xrecv[side(d), j, 0].astype(F32)
            )

    for e in (-1, 1):
        @pl.when(has_z(e))
        def _():
            z_copy(e).wait_send()
            z_copy(e, True).wait_recv()
    for d in (-1, 1):
        for e in (-1, 1):
            @pl.when(jnp.logical_and(has_x(d), has_z(e)))
            def _():
                e_copy(d, e).wait_send()
                e_copy(d, e, True).wait_recv()

    for e in (-1, 1):
        at = jnp.clip(w + e, 0, nw - 1)
        for s in range(live):
            target = jnp.where(has_z(e), own[s], FAR)
            for d in (0, -1, 1):
                ids = idrecv[1 + d, at]
                if d == 0:
                    where_x = slice(1, edge + 1)
                    shape = (edge, edge, chans)
                    value = lambda j: zrecv[side(e), j].astype(F32)
                else:
                    where_x = slice(0, 1) if d < 0 else slice(edge + 1, edge + 2)
                    shape = (1, edge, chans)
                    value = lambda j: erecv[side(d), side(e), j].astype(F32)[None]
                zpad[s, side(e), where_x, 1 : edge + 1, :] = picked(ids, target, shape, value)
                zpad[s, side(e), where_x, 0:1, :] = picked(ids, target - 1, shape, value)[
                    :, edge - 1 : edge
                ]
                zpad[s, side(e), where_x, edge + 1 : edge + 2, :] = picked(
                    ids, target + 1, shape, value
                )[:, 0:1]

    pad = edge + 2
    half = edge // 2
    reach = half + 2
    zrow = lax.broadcasted_iota(jnp.int32, (pad, edge, chans), 1)

    def build(step, carry):
        s = step // reach
        xl = step % reach
        low, mid, high = [], [], []
        for xh in range(2):
            px = xl + half * xh
            v = vol[s, px].reshape(pad, edge, chans)
            below = jnp.broadcast_to(zpad[s, 0, px, 0:pad, :][:, None, :], (pad, edge, chans))
            above = jnp.broadcast_to(zpad[s, 1, px, 0:pad, :][:, None, :], (pad, edge, chans))
            low.append(jnp.where(zrow == 0, below, pltpu.roll(v, 1, axis=1)))
            mid.append(v)
            high.append(jnp.where(zrow == edge - 1, above, pltpu.roll(v, edge - 1, axis=1)))
        for c, pair in enumerate((low, mid, high)):
            cols_lhs[s, xl, :, :, c * chans : (c + 1) * chans] = jnp.concatenate(
                pair, axis=1
            ).astype(BF16)
        return carry

    lax.fori_loop(0, live * reach, build, 0)

    for d, peer in peers:
        @pl.when(far(d, peer))
        def _():
            id_copy(d, peer).start()

    load_w3.wait()
    rows = edge * edge * edge
    out_row = lax.broadcasted_iota(jnp.int32, (last, rows), 0)
    in_row = lax.broadcasted_iota(jnp.int32, (last, rows), 1)
    in_pair = in_row // edge
    in_y = (in_pair // 2) % edge
    in_x = in_pair // (2 * edge) + half * (in_pair % 2)
    pool = jnp.where(in_x * edge + in_y == out_row, 1.0, 0.0).astype(BF16)

    def c_copy(d, peer, s, arrival=False):
        src = csend.at[s] if d == 0 else csend.at[s, 0 if d < 0 else edge - 1]
        if arrival:
            dst = crecv.at[peer, s] if d == 0 else xedge.at[side(d), peer, s]
            sem = c_r.at[1 + d, peer, s]
        else:
            dst = crecv.at[w, s] if d == 0 else xedge.at[side(-d), w, s]
            sem = c_r.at[1 - d, w, s]
        return pltpu.make_async_remote_copy(
            src_ref=src, dst_ref=dst, send_sem=c_s.at[1 + d, peer, s], recv_sem=sem,
            device_id=(g + d, peer), device_id_type=MESH,
        )

    def conv(s, carry):
        acc = jnp.zeros((rows, chans), F32)
        for a in range(3):
            for b in range(3):
                window = cols_lhs[s, pl.ds(a, half), pl.ds(b, edge)].reshape(rows, 3 * chans)
                acc = acc + jnp.dot(window, w3[3 * a + b], preferred_element_type=F32)
        center = cols_lhs[s, pl.ds(1, half), pl.ds(1, edge), :, chans : 2 * chans]
        block = acc * scale3_ref[...] + bias3_ref[...] + center.reshape(rows, chans).astype(F32)
        block = jnp.maximum(block, 0.0).astype(BF16)
        summed = jnp.dot(pool, block, preferred_element_type=F32)
        live_row = ids_ref[0, first + s]
        keep = jnp.full((last, chans), live_row, jnp.int32) < BY
        summed = jnp.where(keep, summed, 0.0).reshape(edge, edge, chans).astype(BF16)
        csend[s] = summed
        crecv[w, s] = summed
        for d, peer in peers:
            @pl.when(present(d, peer))
            def _():
                c_copy(d, peer, s).start()
        return carry

    lax.fori_loop(0, live, conv, 0)

    load_w2.wait()
    for d, peer in peers:
        @pl.when(far(d, peer))
        def _():
            id_copy(d, peer).wait_send()
            id_arrival(d, peer).wait_recv()
        for s in range(live):
            @pl.when(present(d, peer))
            def _():
                c_copy(d, peer, s).wait_send()
                c_copy(d, peer, s, True).wait_recv()

    off = edge
    for d in (0, -1, 1):
        where_x = slice(1, edge + 1) if d == 0 else (slice(0, 1) if d < 0 else slice(edge + 1, edge + 2))
        shape = (edge if d == 0 else 1, edge, chans)
        for q in range(-1, per_slab + 1):
            total = jnp.zeros(shape, F32)
            for peer in range(nw):
                ids = idrecv[1 + d, peer]
                for j in range(live):
                    wide = jnp.concatenate([ids[j : j + 1]] * 2, axis=1)
                    hit = jnp.broadcast_to(wide.reshape(1, 1, chans), shape)
                    if d == 0:
                        value = crecv[peer, j].astype(F32)
                    else:
                        value = xedge[side(d), peer, j].astype(F32)[None]
                    total = total + jnp.where(hit == w * per_slab + q, value, 0.0)
            scale = lax.rsqrt(jnp.mean(total * total, axis=-1, keepdims=True) + 1e-05)
            normed = total * scale * gain_ref[...].reshape(1, 1, chans)
            begin = off + q * edge
            plane[where_x, begin : begin + edge, :] = normed

    for c in range(3):
        lhs2[:, :, c * chans : (c + 1) * chans] = plane[
            :, off + c - 1 : off + c - 1 + ydev, :
        ].astype(BF16)
    total = jnp.zeros((edge * ydev, chans), F32)
    for a in range(3):
        total = total + jnp.dot(
            lhs2[a : a + edge].reshape(edge * ydev, 3 * chans), w2[a], preferred_element_type=F32
        )
    residual = lhs2[1 : edge + 1, :, chans : 2 * chans].reshape(edge * ydev, chans).astype(F32)
    result = jnp.maximum(total * scale2_ref[...] + bias2_ref[...], 0.0) + residual
    out_ref[...] = result.reshape(edge, ydev, chans).astype(BF16)


def per_device(
    ng, nw,
    feats, brick_ids, conv3_w, conv3_scale, conv3_bias, bev_gain, conv2_w, conv2_scale, conv2_bias,
):
    slots, edge, chans = feats.shape[1], feats.shape[2], feats.shape[-1]
    live = slots - 1
    ydev = BY * edge // nw
    pad = edge + 2
    reach = edge // 2 + 2
    vmem = pl.BlockSpec(memory_space=pltpu.VMEM)
    hbm = pl.BlockSpec(memory_space=pl.ANY)
    dma = pltpu.SemaphoreType.DMA
    return pl.pallas_call(
        functools.partial(block_kernel, ng, nw, live),
        out_shape=jax.ShapeDtypeStruct((edge, ydev, chans), BF16),
        in_specs=[pl.BlockSpec(memory_space=pltpu.SMEM), hbm, hbm, hbm] + [vmem] * 5,
        out_specs=vmem,
        scratch_shapes=[
            pltpu.VMEM((live, edge, edge, edge, chans), BF16),
            pltpu.VMEM((live, pad, pad * edge, chans), F32),
            pltpu.VMEM((2, live, edge, edge, chans), BF16),
            pltpu.VMEM((2, live, edge, edge, chans), BF16),
            pltpu.VMEM((2, live, edge, edge, chans), BF16),
            pltpu.VMEM((2, 2, live, edge, chans), BF16),
            pltpu.VMEM((8, chans // 2), jnp.int32),
            pltpu.VMEM((3, nw, 8, chans // 2), jnp.int32),
            pltpu.VMEM((live, 2, pad, 16, chans), F32),
            pltpu.VMEM((live, reach, pad, 2 * edge, 3 * chans), BF16),
            pltpu.VMEM((9, 3 * chans, chans), BF16),
            pltpu.VMEM((3, 3 * chans, chans), BF16),
            pltpu.VMEM((live, edge, edge, chans), BF16),
            pltpu.VMEM((nw, live, edge, edge, chans), BF16),
            pltpu.VMEM((2, nw, live, edge, chans), BF16),
            pltpu.VMEM((pad, ydev + 2 * edge, chans), F32),
            pltpu.VMEM((pad, ydev, 3 * chans), BF16),
            dma((3,)),
            dma((3, nw)), dma((3, nw)),
            dma((2,)), dma((2,)),
            dma((2,)), dma((2,)),
            dma((2, 2)), dma((2, 2)),
            dma((3, nw, live)), dma((3, nw, live)),
        ],
        compiler_params=pltpu.CompilerParams(
            collective_id=0, has_side_effects=True, vmem_limit_bytes=56 << 20
        ),
    )(
        brick_ids,
        feats,
        conv3_w.reshape(9, 3 * chans, chans),
        conv2_w.reshape(3, 3 * chans, chans),
        conv3_scale.reshape(1, chans),
        conv3_bias.reshape(1, chans),
        bev_gain.reshape(1, chans),
        conv2_scale.reshape(1, chans),
        conv2_bias.reshape(1, chans),
    )


def solution(mesh):
    return jax.shard_map(
        functools.partial(per_device, mesh.shape["gx"], mesh.shape["wa"]),
        mesh=mesh,
        in_specs=(
            P("gx", "wa", None, None, None, None),
            P("gx", "wa"),
            P(),
            P(),
            P(),
            P(),
            P(),
            P(),
            P(),
        ),
        out_specs=P("gx", "wa", None),
        check_vma=False,
    )
```

```python
import functools

import jax
import jax.numpy as jnp
from jax import lax
from jax.experimental import pallas as pl
from jax.experimental.pallas import tpu as pltpu
from jax.sharding import PartitionSpec as P

BY = 16
GONE = -99
FAR = -1000
MESH = pl.DeviceIdType.MESH
F32 = jnp.float32
BF16 = jnp.bfloat16


def side(sign):
    return 0 if sign < 0 else 1


def block_kernel(
    ng, nw, live,
    ids_ref, feats_ref, w3_ref, w2_ref, scale3_ref, bias3_ref, gain_ref, scale2_ref, bias2_ref,
    out_ref,
    tiles, vol, zsend, zrecv, xrecv, erecv, idsend, idrecv, zpad, cols_lhs, w3, w2,
    csend, crecv, xedge, plane, lhs2,
    load_sem, id_s, id_r, x_s, x_r, z_s, z_r, e_s, e_r, c_s, c_r,
):
    g = lax.axis_index("gx")
    w = lax.axis_index("wa")
    edge = tiles.shape[1]
    chans = tiles.shape[-1]
    ydev = out_ref.shape[1]
    per_slab = ydev // edge
    first = jnp.where(w < nw // 2, 0, feats_ref.shape[1] - live)

    def has_x(d):
        return jnp.logical_and(g + d >= 0, g + d < ng)

    def has_z(e):
        return jnp.logical_and(w + e >= 0, w + e < nw)

    def present(d, peer):
        return has_x(d) if d else w != peer

    peers = [(d, peer) for d in (0, -1, 1) for peer in range(nw)]

    def near(d, peer):
        return jnp.logical_and(present(d, peer), jnp.abs(w - peer) <= 1)

    def far(d, peer):
        return jnp.logical_and(present(d, peer), jnp.abs(w - peer) > 1)

    load = pltpu.make_async_copy(feats_ref.at[0, pl.ds(first, live)], tiles, load_sem.at[0])
    load.start()
    load_w3 = pltpu.make_async_copy(w3_ref, w3, load_sem.at[1])
    load_w3.start()
    load_w2 = pltpu.make_async_copy(w2_ref, w2, load_sem.at[2])
    load_w2.start()

    barrier = pltpu.get_barrier_semaphore()
    for d, peer in peers:
        @pl.when(present(d, peer))
        def _():
            pl.semaphore_signal(barrier, inc=1, device_id=(g + d, peer), device_id_type=MESH)

    own = [ids_ref[0, first + j] for j in range(live)]
    row = lax.broadcasted_iota(jnp.int32, idsend.shape, 0)
    listed = jnp.full(idsend.shape, GONE, jnp.int32)
    for j in range(live):
        listed = jnp.where(row == j, jnp.where(own[j] < BY, own[j], GONE), listed)
    idsend[...] = listed
    idrecv[1, w] = listed
    for d in (-1, 1):
        @pl.when(jnp.logical_not(has_x(d)))
        def _():
            for peer in range(nw):
                idrecv[1 + d, peer] = jnp.full(idsend.shape, GONE, jnp.int32)

    load.wait()
    for s in range(live):
        vol[s, 1 : edge + 1, edge : edge * (edge + 1), :] = (
            tiles[s].astype(F32).reshape(edge, edge * edge, chans)
        )
    for s in range(live):
        for e, z in ((-1, 0), (1, edge - 1)):
            zsend[side(e), s] = tiles[s].astype(F32)[:, :, z, :].astype(BF16)

    count = (1 + has_x(-1).astype(jnp.int32) + has_x(1).astype(jnp.int32)) * nw - 1
    pl.semaphore_wait(barrier, count)

    def id_copy(d, peer):
        return pltpu.make_async_remote_copy(
            src_ref=idsend, dst_ref=idrecv.at[1 - d, w],
            send_sem=id_s.at[1 + d, peer], recv_sem=id_r.at[1 - d, w],
            device_id=(g + d, peer), device_id_type=MESH,
        )

    def id_arrival(d, peer):
        return pltpu.make_async_remote_copy(
            src_ref=idsend, dst_ref=idrecv.at[1 + d, peer],
            send_sem=id_s.at[1 + d, peer], recv_sem=id_r.at[1 + d, peer],
            device_id=(g + d, peer), device_id_type=MESH,
        )

    def x_copy(d, arrival=False):
        to = side(d) if arrival else side(-d)
        return pltpu.make_async_remote_copy(
            src_ref=tiles.at[:, 0 if d < 0 else edge - 1], dst_ref=xrecv.at[to],
            send_sem=x_s.at[side(d)], recv_sem=x_r.at[to],
            device_id=(g + d, w), device_id_type=MESH,
        )

    def z_copy(e, arrival=False):
        to = side(e) if arrival else side(-e)
        return pltpu.make_async_remote_copy(
            src_ref=zsend.at[side(e)], dst_ref=zrecv.at[to],
            send_sem=z_s.at[side(e)], recv_sem=z_r.at[to],
            device_id=(g, w + e), device_id_type=MESH,
        )

    def e_copy(d, e, arrival=False):
        tx, tz = (side(d), side(e)) if arrival else (side(-d), side(-e))
        return pltpu.make_async_remote_copy(
            src_ref=zsend.at[side(e), :, 0 if d < 0 else edge - 1], dst_ref=erecv.at[tx, tz],
            send_sem=e_s.at[side(d), side(e)], recv_sem=e_r.at[tx, tz],
            device_id=(g + d, w + e), device_id_type=MESH,
        )

    for e in (-1, 1):
        @pl.when(has_z(e))
        def _():
            z_copy(e).start()
    for d in (-1, 1):
        @pl.when(has_x(d))
        def _():
            x_copy(d).start()
    for d in (-1, 1):
        for e in (-1, 1):
            @pl.when(jnp.logical_and(has_x(d), has_z(e)))
            def _():
                e_copy(d, e).start()
    for d, peer in peers:
        @pl.when(near(d, peer))
        def _():
            id_copy(d, peer).start()

    def picked(ids, target, shape, value):
        total = jnp.zeros(shape, F32)
        for j in range(live):
            wide = jnp.concatenate([ids[j : j + 1]] * 2, axis=1)
            hit = jnp.broadcast_to(wide.reshape((1,) * (len(shape) - 1) + (chans,)), shape)
            total = jnp.where(hit == target, value(j), total)
        return total

    last = edge * edge
    for s in range(live):
        vol[s, 1 : edge + 1, 0:edge, :] = picked(
            listed, own[s] - 1, (edge, edge, chans), lambda j: vol[j, 1 : edge + 1, last : last + edge, :]
        )
        vol[s, 1 : edge + 1, last + edge : last + 2 * edge, :] = picked(
            listed, own[s] + 1, (edge, edge, chans), lambda j: vol[j, 1 : edge + 1, edge : 2 * edge, :]
        )

    for d, peer in peers:
        @pl.when(near(d, peer))
        def _():
            id_copy(d, peer).wait_send()
            id_arrival(d, peer).wait_recv()
    for d in (-1, 1):
        @pl.when(has_x(d))
        def _():
            x_copy(d).wait_send()
            x_copy(d, True).wait_recv()

    for e in (-1, 1):
        @pl.when(has_z(e))
        def _():
            z_copy(e).wait_send()
            z_copy(e, True).wait_recv()
    for d in (-1, 1):
        for e in (-1, 1):
            @pl.when(jnp.logical_and(has_x(d), has_z(e)))
            def _():
                e_copy(d, e).wait_send()
                e_copy(d, e, True).wait_recv()

    def place(s):
        mine = ids_ref[0, first + s]
        for d in (-1, 1):
            ids = idrecv[1 + d, w]
            px = 0 if d < 0 else edge + 1
            vol[s, px, edge : last + edge, :] = picked(
                ids, mine, (edge, edge, chans), lambda j: xrecv[side(d), j].astype(F32)
            ).reshape(last, chans)
            vol[s, px, 0:edge, :] = picked(
                ids, mine - 1, (edge, chans), lambda j: xrecv[side(d), j, edge - 1].astype(F32)
            )
            vol[s, px, last + edge : last + 2 * edge, :] = picked(
                ids, mine + 1, (edge, chans), lambda j: xrecv[side(d), j, 0].astype(F32)
            )
        for e in (-1, 1):
            at = jnp.clip(w + e, 0, nw - 1)
            target = jnp.where(has_z(e), mine, FAR)
            for d in (0, -1, 1):
                ids = idrecv[1 + d, at]
                if d == 0:
                    where_x = slice(1, edge + 1)
                    shape = (edge, edge, chans)
                    value = lambda j: zrecv[side(e), j].astype(F32)
                else:
                    where_x = slice(0, 1) if d < 0 else slice(edge + 1, edge + 2)
                    shape = (1, edge, chans)
                    value = lambda j: erecv[side(d), side(e), j].astype(F32)[None]
                zpad[s, side(e), where_x, 1 : edge + 1, :] = picked(ids, target, shape, value)
                zpad[s, side(e), where_x, 0:1, :] = picked(ids, target - 1, shape, value)[
                    :, edge - 1 : edge
                ]
                zpad[s, side(e), where_x, edge + 1 : edge + 2, :] = picked(
                    ids, target + 1, shape, value
                )[:, 0:1]

    pad = edge + 2
    half = edge // 2
    reach = half + 2
    zrow = lax.broadcasted_iota(jnp.int32, (pad, edge, chans), 1)

    def build(xl, s):
        low, mid, high = [], [], []
        for xh in range(2):
            px = xl + half * xh
            v = vol[s, px].reshape(pad, edge, chans)
            below = jnp.broadcast_to(zpad[s, 0, px, 0:pad, :][:, None, :], (pad, edge, chans))
            above = jnp.broadcast_to(zpad[s, 1, px, 0:pad, :][:, None, :], (pad, edge, chans))
            low.append(jnp.where(zrow == 0, below, pltpu.roll(v, 1, axis=1)))
            mid.append(v)
            high.append(jnp.where(zrow == edge - 1, above, pltpu.roll(v, edge - 1, axis=1)))
        for c, pair in enumerate((low, mid, high)):
            cols_lhs[s, xl, :, :, c * chans : (c + 1) * chans] = jnp.concatenate(
                pair, axis=1
            ).astype(BF16)
        return s

    for d, peer in peers:
        @pl.when(far(d, peer))
        def _():
            id_copy(d, peer).start()

    load_w3.wait()
    cut = half // 2
    rows = cut * edge * 2 * edge
    out_row = lax.broadcasted_iota(jnp.int32, (2 * cut * edge, rows), 0)
    in_row = lax.broadcasted_iota(jnp.int32, (2 * cut * edge, rows), 1)
    in_pair = in_row // edge
    in_y = (in_pair // 2) % edge
    in_x = 2 * (in_pair // (2 * edge)) + in_pair % 2
    pool = jnp.where(in_x * edge + in_y == out_row, 1.0, 0.0).astype(BF16)

    def c_copy(d, peer, s, h, arrival=False):
        if d == 0:
            src, mark = csend.at[s, h], h
        else:
            src, mark = csend.at[s, h, 0 if d < 0 else 2 * cut - 1], 0
        if arrival:
            dst = crecv.at[peer, s, h] if d == 0 else xedge.at[side(d), peer, s]
            sem = c_r.at[1 + d, peer, s, mark]
        else:
            dst = crecv.at[w, s, h] if d == 0 else xedge.at[side(-d), w, s]
            sem = c_r.at[1 - d, w, s, mark]
        return pltpu.make_async_remote_copy(
            src_ref=src, dst_ref=dst, send_sem=c_s.at[1 + d, peer, s, mark], recv_sem=sem,
            device_id=(g + d, peer), device_id_type=MESH,
        )

    def parts(d):
        return (0, 1) if d == 0 else ((0,) if d < 0 else (1,))

    def conv(s, carry):
        place(s)
        lax.fori_loop(0, reach, build, s)
        live_row = ids_ref[0, first + s]
        keep = jnp.full((2 * cut * edge, chans), live_row, jnp.int32) < BY
        for h in range(2):
            acc = jnp.zeros((rows, chans), F32)
            for a in range(3):
                for b in range(3):
                    window = cols_lhs[s, pl.ds(a + h * cut, cut), pl.ds(b, edge)]
                    acc = acc + jnp.dot(
                        window.reshape(rows, 3 * chans), w3[3 * a + b], preferred_element_type=F32
                    )
            center = cols_lhs[s, pl.ds(1 + h * cut, cut), pl.ds(1, edge), :, chans : 2 * chans]
            block = acc * scale3_ref[...] + bias3_ref[...] + center.reshape(rows, chans).astype(F32)
            block = jnp.maximum(block, 0.0).astype(BF16)
            summed = jnp.dot(pool, block, preferred_element_type=F32)
            summed = jnp.where(keep, summed, 0.0).reshape(2 * cut, edge, chans).astype(BF16)
            csend[s, h] = summed
            crecv[w, s, h] = summed
            for d, peer in peers:
                if h in parts(d):
                    @pl.when(present(d, peer))
                    def _():
                        c_copy(d, peer, s, h).start()
        return carry

    lax.fori_loop(0, live, conv, 0)

    load_w2.wait()
    for d, peer in peers:
        @pl.when(far(d, peer))
        def _():
            id_copy(d, peer).wait_send()
            id_arrival(d, peer).wait_recv()
        @pl.when(present(d, peer))
        def _():
            for s in range(live):
                for h in parts(d):
                    c_copy(d, peer, s, h).wait_send()
                    c_copy(d, peer, s, h, True).wait_recv()

    off = edge
    for d in (0, -1, 1):
        shape = (edge if d == 0 else 1, edge, chans)
        for q in range(-1, per_slab + 1):
            total = jnp.zeros(shape, F32)
            for peer in range(nw):
                ids = idrecv[1 + d, peer]
                for j in range(live):
                    wide = jnp.concatenate([ids[j : j + 1]] * 2, axis=1)
                    hit = jnp.broadcast_to(wide.reshape(1, 1, chans), shape)
                    if d == 0:
                        value = crecv[peer, j].reshape(shape).astype(F32)
                    else:
                        value = xedge[side(d), peer, j].astype(F32)[None]
                    total = total + jnp.where(hit == w * per_slab + q, value, 0.0)
            scale = lax.rsqrt(jnp.mean(total * total, axis=-1, keepdims=True) + 1e-05)
            normed = total * scale * gain_ref[...].reshape(1, 1, chans)
            begin = off + q * edge
            for r in range(shape[0]):
                if d == 0:
                    px = 1 + (r // (2 * cut)) * cut + (r % (2 * cut)) // 2 + half * (r % 2)
                else:
                    px = 0 if d < 0 else edge + 1
                plane[px, begin : begin + edge, :] = normed[r]

    for c in range(3):
        lhs2[:, :, c * chans : (c + 1) * chans] = plane[
            :, off + c - 1 : off + c - 1 + ydev, :
        ].astype(BF16)
    total = jnp.zeros((edge * ydev, chans), F32)
    for a in range(3):
        total = total + jnp.dot(
            lhs2[a : a + edge].reshape(edge * ydev, 3 * chans), w2[a], preferred_element_type=F32
        )
    residual = lhs2[1 : edge + 1, :, chans : 2 * chans].reshape(edge * ydev, chans).astype(F32)
    result = jnp.maximum(total * scale2_ref[...] + bias2_ref[...], 0.0) + residual
    out_ref[...] = result.reshape(edge, ydev, chans).astype(BF16)


def per_device(
    ng, nw,
    feats, brick_ids, conv3_w, conv3_scale, conv3_bias, bev_gain, conv2_w, conv2_scale, conv2_bias,
):
    slots, edge, chans = feats.shape[1], feats.shape[2], feats.shape[-1]
    live = slots - 1
    ydev = BY * edge // nw
    pad = edge + 2
    reach = edge // 2 + 2
    vmem = pl.BlockSpec(memory_space=pltpu.VMEM)
    hbm = pl.BlockSpec(memory_space=pl.ANY)
    dma = pltpu.SemaphoreType.DMA
    return pl.pallas_call(
        functools.partial(block_kernel, ng, nw, live),
        out_shape=jax.ShapeDtypeStruct((edge, ydev, chans), BF16),
        in_specs=[pl.BlockSpec(memory_space=pltpu.SMEM), hbm, hbm, hbm] + [vmem] * 5,
        out_specs=vmem,
        scratch_shapes=[
            pltpu.VMEM((live, edge, edge, edge, chans), BF16),
            pltpu.VMEM((live, pad, pad * edge, chans), F32),
            pltpu.VMEM((2, live, edge, edge, chans), BF16),
            pltpu.VMEM((2, live, edge, edge, chans), BF16),
            pltpu.VMEM((2, live, edge, edge, chans), BF16),
            pltpu.VMEM((2, 2, live, edge, chans), BF16),
            pltpu.VMEM((8, chans // 2), jnp.int32),
            pltpu.VMEM((3, nw, 8, chans // 2), jnp.int32),
            pltpu.VMEM((live, 2, pad, 16, chans), F32),
            pltpu.VMEM((live, reach, pad, 2 * edge, 3 * chans), BF16),
            pltpu.VMEM((9, 3 * chans, chans), BF16),
            pltpu.VMEM((3, 3 * chans, chans), BF16),
            pltpu.VMEM((live, 2, edge // 2, edge, chans), BF16),
            pltpu.VMEM((nw, live, 2, edge // 2, edge, chans), BF16),
            pltpu.VMEM((2, nw, live, edge, chans), BF16),
            pltpu.VMEM((pad, ydev + 2 * edge, chans), F32),
            pltpu.VMEM((pad, ydev, 3 * chans), BF16),
            dma((3,)),
            dma((3, nw)), dma((3, nw)),
            dma((2,)), dma((2,)),
            dma((2,)), dma((2,)),
            dma((2, 2)), dma((2, 2)),
            dma((3, nw, live, 2)), dma((3, nw, live, 2)),
        ],
        compiler_params=pltpu.CompilerParams(
            collective_id=0, has_side_effects=True, vmem_limit_bytes=56 << 20
        ),
    )(
        brick_ids,
        feats,
        conv3_w.reshape(9, 3 * chans, chans),
        conv2_w.reshape(3, 3 * chans, chans),
        conv3_scale.reshape(1, chans),
        conv3_bias.reshape(1, chans),
        bev_gain.reshape(1, chans),
        conv2_scale.reshape(1, chans),
        conv2_bias.reshape(1, chans),
    )


def solution(mesh):
    return jax.shard_map(
        functools.partial(per_device, mesh.shape["gx"], mesh.shape["wa"]),
        mesh=mesh,
        in_specs=(
            P("gx", "wa", None, None, None, None),
            P("gx", "wa"),
            P(),
            P(),
            P(),
            P(),
            P(),
            P(),
            P(),
        ),
        out_specs=P("gx", "wa", None),
        check_vma=False,
    )
```

```python
import functools

import jax
import jax.numpy as jnp
from jax import lax
from jax.experimental import pallas as pl
from jax.experimental.pallas import tpu as pltpu
from jax.sharding import PartitionSpec as P

BY = 16
GONE = -99
FAR = -1000
MESH = pl.DeviceIdType.MESH
F32 = jnp.float32
BF16 = jnp.bfloat16


def side(sign):
    return 0 if sign < 0 else 1


def block_kernel(
    ng, nw, live,
    ids_ref, feats_ref, w3_ref, w2_ref, scale3_ref, bias3_ref, gain_ref, scale2_ref, bias2_ref,
    out_ref,
    tiles, vol, zsend, zrecv, xrecv, erecv, idsend, idrecv, zpad, cols_lhs, w3, w2,
    csend, crecv, xedge, plane, lhs2,
    load_sem, id_s, id_r, x_s, x_r, z_s, z_r, e_s, e_r, c_s, c_r,
):
    g = lax.axis_index("gx")
    w = lax.axis_index("wa")
    edge = tiles.shape[1]
    chans = tiles.shape[-1]
    ydev = out_ref.shape[1]
    per_slab = ydev // edge
    first = jnp.where(w < nw // 2, 0, feats_ref.shape[1] - live)

    def has_x(d):
        return jnp.logical_and(g + d >= 0, g + d < ng)

    def has_z(e):
        return jnp.logical_and(w + e >= 0, w + e < nw)

    def present(d, peer):
        return has_x(d) if d else w != peer

    peers = [(d, peer) for d in (0, -1, 1) for peer in range(nw)]

    def near(d, peer):
        return jnp.logical_and(present(d, peer), jnp.abs(w - peer) <= 1)

    def far(d, peer):
        return jnp.logical_and(present(d, peer), jnp.abs(w - peer) > 1)

    load = pltpu.make_async_copy(feats_ref.at[0, pl.ds(first, live)], tiles, load_sem.at[0])
    load.start()
    load_w3 = pltpu.make_async_copy(w3_ref, w3, load_sem.at[1])
    load_w3.start()
    load_w2 = pltpu.make_async_copy(w2_ref, w2, load_sem.at[2])
    load_w2.start()

    barrier = pltpu.get_barrier_semaphore()
    for d, peer in peers:
        @pl.when(present(d, peer))
        def _():
            pl.semaphore_signal(barrier, inc=1, device_id=(g + d, peer), device_id_type=MESH)

    own = [ids_ref[0, first + j] for j in range(live)]
    row = lax.broadcasted_iota(jnp.int32, idsend.shape, 0)
    listed = jnp.full(idsend.shape, GONE, jnp.int32)
    for j in range(live):
        listed = jnp.where(row == j, jnp.where(own[j] < BY, own[j], GONE), listed)
    idsend[...] = listed
    idrecv[1, w] = listed
    for d in (-1, 1):
        @pl.when(jnp.logical_not(has_x(d)))
        def _():
            for peer in range(nw):
                idrecv[1 + d, peer] = jnp.full(idsend.shape, GONE, jnp.int32)

    load.wait()
    for s in range(live):
        vol[s, 1 : edge + 1, edge : edge * (edge + 1), :] = (
            tiles[s].astype(F32).reshape(edge, edge * edge, chans)
        )
    for s in range(live):
        for e, z in ((-1, 0), (1, edge - 1)):
            zsend[side(e), s] = tiles[s].astype(F32)[:, :, z, :].astype(BF16)

    count = (1 + has_x(-1).astype(jnp.int32) + has_x(1).astype(jnp.int32)) * nw - 1
    pl.semaphore_wait(barrier, count)

    def id_copy(d, peer):
        return pltpu.make_async_remote_copy(
            src_ref=idsend, dst_ref=idrecv.at[1 - d, w],
            send_sem=id_s.at[1 + d, peer], recv_sem=id_r.at[1 - d, w],
            device_id=(g + d, peer), device_id_type=MESH,
        )

    def id_arrival(d, peer):
        return pltpu.make_async_remote_copy(
            src_ref=idsend, dst_ref=idrecv.at[1 + d, peer],
            send_sem=id_s.at[1 + d, peer], recv_sem=id_r.at[1 + d, peer],
            device_id=(g + d, peer), device_id_type=MESH,
        )

    def x_copy(d, arrival=False):
        to = side(d) if arrival else side(-d)
        return pltpu.make_async_remote_copy(
            src_ref=tiles.at[:, 0 if d < 0 else edge - 1], dst_ref=xrecv.at[to],
            send_sem=x_s.at[side(d)], recv_sem=x_r.at[to],
            device_id=(g + d, w), device_id_type=MESH,
        )

    def z_copy(e, arrival=False):
        to = side(e) if arrival else side(-e)
        return pltpu.make_async_remote_copy(
            src_ref=zsend.at[side(e)], dst_ref=zrecv.at[to],
            send_sem=z_s.at[side(e)], recv_sem=z_r.at[to],
            device_id=(g, w + e), device_id_type=MESH,
        )

    def e_copy(d, e, arrival=False):
        tx, tz = (side(d), side(e)) if arrival else (side(-d), side(-e))
        return pltpu.make_async_remote_copy(
            src_ref=zsend.at[side(e), :, 0 if d < 0 else edge - 1], dst_ref=erecv.at[tx, tz],
            send_sem=e_s.at[side(d), side(e)], recv_sem=e_r.at[tx, tz],
            device_id=(g + d, w + e), device_id_type=MESH,
        )

    for e in (-1, 1):
        @pl.when(has_z(e))
        def _():
            z_copy(e).start()
    for d in (-1, 1):
        @pl.when(has_x(d))
        def _():
            x_copy(d).start()
    for d in (-1, 1):
        for e in (-1, 1):
            @pl.when(jnp.logical_and(has_x(d), has_z(e)))
            def _():
                e_copy(d, e).start()
    for d, peer in peers:
        @pl.when(near(d, peer))
        def _():
            id_copy(d, peer).start()

    def picked(ids, target, shape, value):
        total = jnp.zeros(shape, F32)
        for j in range(live):
            wide = jnp.concatenate([ids[j : j + 1]] * 2, axis=1)
            hit = jnp.broadcast_to(wide.reshape((1,) * (len(shape) - 1) + (chans,)), shape)
            total = jnp.where(hit == target, value(j), total)
        return total

    last = edge * edge
    for s in range(live):
        vol[s, 1 : edge + 1, 0:edge, :] = picked(
            listed, own[s] - 1, (edge, edge, chans), lambda j: vol[j, 1 : edge + 1, last : last + edge, :]
        )
        vol[s, 1 : edge + 1, last + edge : last + 2 * edge, :] = picked(
            listed, own[s] + 1, (edge, edge, chans), lambda j: vol[j, 1 : edge + 1, edge : 2 * edge, :]
        )

    for d, peer in peers:
        @pl.when(near(d, peer))
        def _():
            id_copy(d, peer).wait_send()
            id_arrival(d, peer).wait_recv()
    for d in (-1, 1):
        @pl.when(has_x(d))
        def _():
            x_copy(d).wait_send()
            x_copy(d, True).wait_recv()

    for e in (-1, 1):
        @pl.when(has_z(e))
        def _():
            z_copy(e).wait_send()
            z_copy(e, True).wait_recv()
    for d in (-1, 1):
        for e in (-1, 1):
            @pl.when(jnp.logical_and(has_x(d), has_z(e)))
            def _():
                e_copy(d, e).wait_send()
                e_copy(d, e, True).wait_recv()

    def place(s):
        mine = ids_ref[0, first + s]
        for d in (-1, 1):
            ids = idrecv[1 + d, w]
            px = 0 if d < 0 else edge + 1
            vol[s, px, edge : last + edge, :] = picked(
                ids, mine, (edge, edge, chans), lambda j: xrecv[side(d), j].astype(F32)
            ).reshape(last, chans)
            vol[s, px, 0:edge, :] = picked(
                ids, mine - 1, (edge, chans), lambda j: xrecv[side(d), j, edge - 1].astype(F32)
            )
            vol[s, px, last + edge : last + 2 * edge, :] = picked(
                ids, mine + 1, (edge, chans), lambda j: xrecv[side(d), j, 0].astype(F32)
            )
        for e in (-1, 1):
            at = jnp.clip(w + e, 0, nw - 1)
            target = jnp.where(has_z(e), mine, FAR)
            for d in (0, -1, 1):
                ids = idrecv[1 + d, at]
                if d == 0:
                    where_x = slice(1, edge + 1)
                    shape = (edge, edge, chans)
                    value = lambda j: zrecv[side(e), j].astype(F32)
                else:
                    where_x = slice(0, 1) if d < 0 else slice(edge + 1, edge + 2)
                    shape = (1, edge, chans)
                    value = lambda j: erecv[side(d), side(e), j].astype(F32)[None]
                zpad[s, side(e), where_x, 1 : edge + 1, :] = picked(ids, target, shape, value)
                zpad[s, side(e), where_x, 0:1, :] = picked(ids, target - 1, shape, value)[
                    :, edge - 1 : edge
                ]
                zpad[s, side(e), where_x, edge + 1 : edge + 2, :] = picked(
                    ids, target + 1, shape, value
                )[:, 0:1]

    pad = edge + 2
    half = edge // 2
    reach = half + 2
    zrow = lax.broadcasted_iota(jnp.int32, (pad, edge, chans), 1)

    def build(xl, s):
        low, mid, high = [], [], []
        for xh in range(2):
            px = xl + half * xh
            v = vol[s, px].reshape(pad, edge, chans)
            below = jnp.broadcast_to(zpad[s, 0, px, 0:pad, :][:, None, :], (pad, edge, chans))
            above = jnp.broadcast_to(zpad[s, 1, px, 0:pad, :][:, None, :], (pad, edge, chans))
            low.append(jnp.where(zrow == 0, below, pltpu.roll(v, 1, axis=1)))
            mid.append(v)
            high.append(jnp.where(zrow == edge - 1, above, pltpu.roll(v, edge - 1, axis=1)))
        for c, pair in enumerate((low, mid, high)):
            cols_lhs[s, xl, :, :, c * chans : (c + 1) * chans] = jnp.concatenate(
                pair, axis=1
            ).astype(BF16)
        return s

    for d, peer in peers:
        @pl.when(far(d, peer))
        def _():
            id_copy(d, peer).start()

    load_w3.wait()
    rows = edge * edge * edge
    out_row = lax.broadcasted_iota(jnp.int32, (last, rows), 0)
    in_row = lax.broadcasted_iota(jnp.int32, (last, rows), 1)
    in_pair = in_row // edge
    in_y = (in_pair // 2) % edge
    in_x = in_pair // (2 * edge) + half * (in_pair % 2)
    pool = jnp.where(in_x * edge + in_y == out_row, 1.0, 0.0).astype(BF16)

    def c_copy(d, peer, s, arrival=False):
        src = csend.at[s] if d == 0 else csend.at[s, 0 if d < 0 else edge - 1]
        if arrival:
            dst = crecv.at[peer, s] if d == 0 else xedge.at[side(d), peer, s]
            sem = c_r.at[1 + d, peer]
        else:
            dst = crecv.at[w, s] if d == 0 else xedge.at[side(-d), w, s]
            sem = c_r.at[1 - d, w]
        return pltpu.make_async_remote_copy(
            src_ref=src, dst_ref=dst, send_sem=c_s.at[1 + d, peer], recv_sem=sem,
            device_id=(g + d, peer), device_id_type=MESH,
        )

    def conv(s, carry):
        place(s)
        lax.fori_loop(0, reach, build, s)
        acc = jnp.zeros((rows, chans), F32)
        for a in range(3):
            for b in range(3):
                window = cols_lhs[s, pl.ds(a, half), pl.ds(b, edge)].reshape(rows, 3 * chans)
                acc = acc + jnp.dot(window, w3[3 * a + b], preferred_element_type=F32)
        center = cols_lhs[s, pl.ds(1, half), pl.ds(1, edge), :, chans : 2 * chans]
        block = acc * scale3_ref[...] + bias3_ref[...] + center.reshape(rows, chans).astype(F32)
        block = jnp.maximum(block, 0.0).astype(BF16)
        summed = jnp.dot(pool, block, preferred_element_type=F32)
        live_row = ids_ref[0, first + s]
        keep = jnp.full((last, chans), live_row, jnp.int32) < BY
        summed = jnp.where(keep, summed, 0.0).reshape(edge, edge, chans).astype(BF16)
        csend[s] = summed
        crecv[w, s] = summed
        for d, peer in peers:
            @pl.when(present(d, peer))
            def _():
                c_copy(d, peer, s).start()
        return carry

    lax.fori_loop(0, live, conv, 0)

    load_w2.wait()
    for d, peer in peers:
        @pl.when(far(d, peer))
        def _():
            id_copy(d, peer).wait_send()
            id_arrival(d, peer).wait_recv()
        @pl.when(present(d, peer))
        def _():
            every = slice(None)
            c_copy(d, peer, every).wait_send()
            c_copy(d, peer, every, True).wait_recv()

    off = edge
    for d in (0, -1, 1):
        where_x = slice(1, edge + 1) if d == 0 else (slice(0, 1) if d < 0 else slice(edge + 1, edge + 2))
        shape = (edge if d == 0 else 1, edge, chans)
        for q in range(-1, per_slab + 1):
            total = jnp.zeros(shape, F32)
            for peer in range(nw):
                ids = idrecv[1 + d, peer]
                for j in range(live):
                    wide = jnp.concatenate([ids[j : j + 1]] * 2, axis=1)
                    hit = jnp.broadcast_to(wide.reshape(1, 1, chans), shape)
                    if d == 0:
                        value = crecv[peer, j].astype(F32)
                    else:
                        value = xedge[side(d), peer, j].astype(F32)[None]
                    total = total + jnp.where(hit == w * per_slab + q, value, 0.0)
            scale = lax.rsqrt(jnp.mean(total * total, axis=-1, keepdims=True) + 1e-05)
            normed = total * scale * gain_ref[...].reshape(1, 1, chans)
            begin = off + q * edge
            plane[where_x, begin : begin + edge, :] = normed

    for c in range(3):
        lhs2[:, :, c * chans : (c + 1) * chans] = plane[
            :, off + c - 1 : off + c - 1 + ydev, :
        ].astype(BF16)
    total = jnp.zeros((edge * ydev, chans), F32)
    for a in range(3):
        total = total + jnp.dot(
            lhs2[a : a + edge].reshape(edge * ydev, 3 * chans), w2[a], preferred_element_type=F32
        )
    residual = lhs2[1 : edge + 1, :, chans : 2 * chans].reshape(edge * ydev, chans).astype(F32)
    result = jnp.maximum(total * scale2_ref[...] + bias2_ref[...], 0.0) + residual
    out_ref[...] = result.reshape(edge, ydev, chans).astype(BF16)


def per_device(
    ng, nw,
    feats, brick_ids, conv3_w, conv3_scale, conv3_bias, bev_gain, conv2_w, conv2_scale, conv2_bias,
):
    slots, edge, chans = feats.shape[1], feats.shape[2], feats.shape[-1]
    live = slots - 1
    ydev = BY * edge // nw
    pad = edge + 2
    reach = edge // 2 + 2
    vmem = pl.BlockSpec(memory_space=pltpu.VMEM)
    hbm = pl.BlockSpec(memory_space=pl.ANY)
    dma = pltpu.SemaphoreType.DMA
    return pl.pallas_call(
        functools.partial(block_kernel, ng, nw, live),
        out_shape=jax.ShapeDtypeStruct((edge, ydev, chans), BF16),
        in_specs=[pl.BlockSpec(memory_space=pltpu.SMEM), hbm, hbm, hbm] + [vmem] * 5,
        out_specs=vmem,
        scratch_shapes=[
            pltpu.VMEM((live, edge, edge, edge, chans), BF16),
            pltpu.VMEM((live, pad, pad * edge, chans), F32),
            pltpu.VMEM((2, live, edge, edge, chans), BF16),
            pltpu.VMEM((2, live, edge, edge, chans), BF16),
            pltpu.VMEM((2, live, edge, edge, chans), BF16),
            pltpu.VMEM((2, 2, live, edge, chans), BF16),
            pltpu.VMEM((8, chans // 2), jnp.int32),
            pltpu.VMEM((3, nw, 8, chans // 2), jnp.int32),
            pltpu.VMEM((live, 2, pad, 16, chans), F32),
            pltpu.VMEM((live, reach, pad, 2 * edge, 3 * chans), BF16),
            pltpu.VMEM((9, 3 * chans, chans), BF16),
            pltpu.VMEM((3, 3 * chans, chans), BF16),
            pltpu.VMEM((live, edge, edge, chans), BF16),
            pltpu.VMEM((nw, live, edge, edge, chans), BF16),
            pltpu.VMEM((2, nw, live, edge, chans), BF16),
            pltpu.VMEM((pad, ydev + 2 * edge, chans), F32),
            pltpu.VMEM((pad, ydev, 3 * chans), BF16),
            dma((3,)),
            dma((3, nw)), dma((3, nw)),
            dma((2,)), dma((2,)),
            dma((2,)), dma((2,)),
            dma((2, 2)), dma((2, 2)),
            dma((3, nw)), dma((3, nw)),
        ],
        compiler_params=pltpu.CompilerParams(
            collective_id=0, has_side_effects=True, vmem_limit_bytes=56 << 20
        ),
    )(
        brick_ids,
        feats,
        conv3_w.reshape(9, 3 * chans, chans),
        conv2_w.reshape(3, 3 * chans, chans),
        conv3_scale.reshape(1, chans),
        conv3_bias.reshape(1, chans),
        bev_gain.reshape(1, chans),
        conv2_scale.reshape(1, chans),
        conv2_bias.reshape(1, chans),
    )


def solution(mesh):
    return jax.shard_map(
        functools.partial(per_device, mesh.shape["gx"], mesh.shape["wa"]),
        mesh=mesh,
        in_specs=(
            P("gx", "wa", None, None, None, None),
            P("gx", "wa"),
            P(),
            P(),
            P(),
            P(),
            P(),
            P(),
            P(),
        ),
        out_specs=P("gx", "wa", None),
        check_vma=False,
    )
```

```python
import functools

import jax
import jax.numpy as jnp
from jax import lax
from jax.experimental import pallas as pl
from jax.experimental.pallas import tpu as pltpu
from jax.sharding import PartitionSpec as P

BY = 16
GONE = -99
FAR = -1000
MESH = pl.DeviceIdType.MESH
F32 = jnp.float32
BF16 = jnp.bfloat16


def side(sign):
    return 0 if sign < 0 else 1


def block_kernel(
    ng, nw, live,
    ids_ref, feats_ref, w3_ref, w2_ref, scale3_ref, bias3_ref, gain_ref, scale2_ref, bias2_ref,
    out_ref,
    tiles, vol, zsend, zrecv, xrecv, erecv, idsend, idrecv, zpad, cols_lhs, w3, w2,
    csend, crecv, xedge, plane, lhs2,
    load_sem, id_s, id_r, x_s, x_r, z_s, z_r, e_s, e_r, c_s, c_r,
):
    g = lax.axis_index("gx")
    w = lax.axis_index("wa")
    edge = tiles.shape[1]
    chans = tiles.shape[-1]
    ydev = out_ref.shape[1]
    per_slab = ydev // edge
    first = jnp.where(w < nw // 2, 0, feats_ref.shape[1] - live)

    def has_x(d):
        return jnp.logical_and(g + d >= 0, g + d < ng)

    def has_z(e):
        return jnp.logical_and(w + e >= 0, w + e < nw)

    def present(d, peer):
        return has_x(d) if d else w != peer

    peers = [(d, peer) for d in (0, -1, 1) for peer in range(nw)]

    def near(d, peer):
        return jnp.logical_and(present(d, peer), jnp.abs(w - peer) <= 1)

    def far(d, peer):
        return jnp.logical_and(present(d, peer), jnp.abs(w - peer) > 1)

    load = pltpu.make_async_copy(feats_ref.at[0, pl.ds(first, live)], tiles, load_sem.at[0])
    load.start()
    load_w3 = pltpu.make_async_copy(w3_ref, w3, load_sem.at[1])
    load_w3.start()
    load_w2 = pltpu.make_async_copy(w2_ref, w2, load_sem.at[2])
    load_w2.start()

    barrier = pltpu.get_barrier_semaphore()
    for d, peer in peers:
        @pl.when(present(d, peer))
        def _():
            pl.semaphore_signal(barrier, inc=1, device_id=(g + d, peer), device_id_type=MESH)

    own = [ids_ref[0, first + j] for j in range(live)]
    row = lax.broadcasted_iota(jnp.int32, idsend.shape, 0)
    listed = jnp.full(idsend.shape, GONE, jnp.int32)
    for j in range(live):
        listed = jnp.where(row == j, jnp.where(own[j] < BY, own[j], GONE), listed)
    idsend[...] = listed
    idrecv[1, w] = listed
    for d in (-1, 1):
        @pl.when(jnp.logical_not(has_x(d)))
        def _():
            for peer in range(nw):
                idrecv[1 + d, peer] = jnp.full(idsend.shape, GONE, jnp.int32)

    load.wait()
    for s in range(live):
        vol[s, 1 : edge + 1, edge : edge * (edge + 1), :] = (
            tiles[s].astype(F32).reshape(edge, edge * edge, chans)
        )
    for s in range(live):
        for e, z in ((-1, 0), (1, edge - 1)):
            zsend[side(e), s] = tiles[s].astype(F32)[:, :, z, :].astype(BF16)

    count = (1 + has_x(-1).astype(jnp.int32) + has_x(1).astype(jnp.int32)) * nw - 1
    pl.semaphore_wait(barrier, count)

    def id_copy(d, peer):
        return pltpu.make_async_remote_copy(
            src_ref=idsend, dst_ref=idrecv.at[1 - d, w],
            send_sem=id_s.at[1 + d, peer], recv_sem=id_r.at[1 - d, w],
            device_id=(g + d, peer), device_id_type=MESH,
        )

    def id_arrival(d, peer):
        return pltpu.make_async_remote_copy(
            src_ref=idsend, dst_ref=idrecv.at[1 + d, peer],
            send_sem=id_s.at[1 + d, peer], recv_sem=id_r.at[1 + d, peer],
            device_id=(g + d, peer), device_id_type=MESH,
        )

    def x_copy(d, arrival=False):
        to = side(d) if arrival else side(-d)
        return pltpu.make_async_remote_copy(
            src_ref=tiles.at[:, 0 if d < 0 else edge - 1], dst_ref=xrecv.at[to],
            send_sem=x_s.at[side(d)], recv_sem=x_r.at[to],
            device_id=(g + d, w), device_id_type=MESH,
        )

    def z_copy(e, arrival=False):
        to = side(e) if arrival else side(-e)
        return pltpu.make_async_remote_copy(
            src_ref=zsend.at[side(e)], dst_ref=zrecv.at[to],
            send_sem=z_s.at[side(e)], recv_sem=z_r.at[to],
            device_id=(g, w + e), device_id_type=MESH,
        )

    def e_copy(d, e, arrival=False):
        tx, tz = (side(d), side(e)) if arrival else (side(-d), side(-e))
        return pltpu.make_async_remote_copy(
            src_ref=zsend.at[side(e), :, 0 if d < 0 else edge - 1], dst_ref=erecv.at[tx, tz],
            send_sem=e_s.at[side(d), side(e)], recv_sem=e_r.at[tx, tz],
            device_id=(g + d, w + e), device_id_type=MESH,
        )

    for e in (-1, 1):
        @pl.when(has_z(e))
        def _():
            z_copy(e).start()
    for d in (-1, 1):
        @pl.when(has_x(d))
        def _():
            x_copy(d).start()
    for d in (-1, 1):
        for e in (-1, 1):
            @pl.when(jnp.logical_and(has_x(d), has_z(e)))
            def _():
                e_copy(d, e).start()
    for d, peer in peers:
        @pl.when(near(d, peer))
        def _():
            id_copy(d, peer).start()

    def picked(ids, target, shape, value):
        total = jnp.zeros(shape, F32)
        for j in range(live):
            wide = jnp.concatenate([ids[j : j + 1]] * 2, axis=1)
            hit = jnp.broadcast_to(wide.reshape((1,) * (len(shape) - 1) + (chans,)), shape)
            total = jnp.where(hit == target, value(j), total)
        return total

    last = edge * edge
    for s in range(live):
        vol[s, 1 : edge + 1, 0:edge, :] = picked(
            listed, own[s] - 1, (edge, edge, chans), lambda j: vol[j, 1 : edge + 1, last : last + edge, :]
        )
        vol[s, 1 : edge + 1, last + edge : last + 2 * edge, :] = picked(
            listed, own[s] + 1, (edge, edge, chans), lambda j: vol[j, 1 : edge + 1, edge : 2 * edge, :]
        )

    for d, peer in peers:
        @pl.when(near(d, peer))
        def _():
            id_copy(d, peer).wait_send()
            id_arrival(d, peer).wait_recv()
    for d in (-1, 1):
        @pl.when(has_x(d))
        def _():
            x_copy(d).wait_send()
            x_copy(d, True).wait_recv()

    for e in (-1, 1):
        @pl.when(has_z(e))
        def _():
            z_copy(e).wait_send()
            z_copy(e, True).wait_recv()
    for d in (-1, 1):
        for e in (-1, 1):
            @pl.when(jnp.logical_and(has_x(d), has_z(e)))
            def _():
                e_copy(d, e).wait_send()
                e_copy(d, e, True).wait_recv()

    def place(s):
        mine = ids_ref[0, first + s]
        for d in (-1, 1):
            ids = idrecv[1 + d, w]
            px = 0 if d < 0 else edge + 1
            vol[s, px, edge : last + edge, :] = picked(
                ids, mine, (edge, edge, chans), lambda j: xrecv[side(d), j].astype(F32)
            ).reshape(last, chans)
            vol[s, px, 0:edge, :] = picked(
                ids, mine - 1, (edge, chans), lambda j: xrecv[side(d), j, edge - 1].astype(F32)
            )
            vol[s, px, last + edge : last + 2 * edge, :] = picked(
                ids, mine + 1, (edge, chans), lambda j: xrecv[side(d), j, 0].astype(F32)
            )
        for e in (-1, 1):
            at = jnp.clip(w + e, 0, nw - 1)
            target = jnp.where(has_z(e), mine, FAR)
            for d in (0, -1, 1):
                ids = idrecv[1 + d, at]
                if d == 0:
                    where_x = slice(1, edge + 1)
                    shape = (edge, edge, chans)
                    value = lambda j: zrecv[side(e), j].astype(F32)
                else:
                    where_x = slice(0, 1) if d < 0 else slice(edge + 1, edge + 2)
                    shape = (1, edge, chans)
                    value = lambda j: erecv[side(d), side(e), j].astype(F32)[None]
                zpad[s, side(e), where_x, 1 : edge + 1, :] = picked(ids, target, shape, value)
                zpad[s, side(e), where_x, 0:1, :] = picked(ids, target - 1, shape, value)[
                    :, edge - 1 : edge
                ]
                zpad[s, side(e), where_x, edge + 1 : edge + 2, :] = picked(
                    ids, target + 1, shape, value
                )[:, 0:1]

    pad = edge + 2
    half = edge // 2
    reach = half + 2
    zrow = lax.broadcasted_iota(jnp.int32, (pad, edge, chans), 1)

    def build(xl, s):
        low, mid, high = [], [], []
        for xh in range(2):
            px = xl + half * xh
            v = vol[s, px].reshape(pad, edge, chans)
            below = jnp.broadcast_to(zpad[s, 0, px, 0:pad, :][:, None, :], (pad, edge, chans))
            above = jnp.broadcast_to(zpad[s, 1, px, 0:pad, :][:, None, :], (pad, edge, chans))
            low.append(jnp.where(zrow == 0, below, pltpu.roll(v, 1, axis=1)))
            mid.append(v)
            high.append(jnp.where(zrow == edge - 1, above, pltpu.roll(v, edge - 1, axis=1)))
        for c, pair in enumerate((low, mid, high)):
            cols_lhs[s, xl, :, :, c * chans : (c + 1) * chans] = jnp.concatenate(
                pair, axis=1
            ).astype(BF16)
        return s

    for d, peer in peers:
        @pl.when(far(d, peer))
        def _():
            id_copy(d, peer).start()

    load_w3.wait()
    rows = edge * edge * edge
    out_row = lax.broadcasted_iota(jnp.int32, (last, rows), 0)
    in_row = lax.broadcasted_iota(jnp.int32, (last, rows), 1)
    in_pair = in_row // edge
    in_y = (in_pair // 2) % edge
    in_x = in_pair // (2 * edge) + half * (in_pair % 2)
    pool = jnp.where(in_x * edge + in_y == out_row, 1.0, 0.0).astype(BF16)

    def c_copy(d, peer, s, arrival=False):
        src = csend.at[s] if d == 0 else csend.at[s, 0 if d < 0 else edge - 1]
        if arrival:
            dst = crecv.at[peer, s] if d == 0 else xedge.at[side(d), peer, s]
            sem = c_r.at[1 + d, peer]
        else:
            dst = crecv.at[w, s] if d == 0 else xedge.at[side(-d), w, s]
            sem = c_r.at[1 - d, w]
        return pltpu.make_async_remote_copy(
            src_ref=src, dst_ref=dst, send_sem=c_s.at[1 + d, peer], recv_sem=sem,
            device_id=(g + d, peer), device_id_type=MESH,
        )

    def conv(s, carry):
        place(s)
        lax.fori_loop(0, reach, build, s, unroll=2)
        acc = jnp.zeros((rows, chans), F32)
        for a in range(3):
            for b in range(3):
                window = cols_lhs[s, pl.ds(a, half), pl.ds(b, edge)].reshape(rows, 3 * chans)
                acc = acc + jnp.dot(window, w3[3 * a + b], preferred_element_type=F32)
        center = cols_lhs[s, pl.ds(1, half), pl.ds(1, edge), :, chans : 2 * chans]
        block = acc * scale3_ref[...] + bias3_ref[...] + center.reshape(rows, chans).astype(F32)
        block = jnp.maximum(block, 0.0).astype(BF16)
        summed = jnp.dot(pool, block, preferred_element_type=F32)
        live_row = ids_ref[0, first + s]
        keep = jnp.full((last, chans), live_row, jnp.int32) < BY
        summed = jnp.where(keep, summed, 0.0).reshape(edge, edge, chans).astype(BF16)
        csend[s] = summed
        crecv[w, s] = summed
        for peer in range(nw):
            @pl.when(present(0, peer))
            def _():
                c_copy(0, peer, s).start()
        for d in (-1, 1):
            @pl.when(has_x(d))
            def _():
                for peer in range(nw):
                    c_copy(d, peer, s).start()
        return carry

    lax.fori_loop(0, live, conv, 0)

    load_w2.wait()
    for d, peer in peers:
        @pl.when(far(d, peer))
        def _():
            id_copy(d, peer).wait_send()
            id_arrival(d, peer).wait_recv()
        @pl.when(present(d, peer))
        def _():
            every = slice(None)
            c_copy(d, peer, every).wait_send()
            c_copy(d, peer, every, True).wait_recv()

    off = edge
    for d in (0, -1, 1):
        where_x = slice(1, edge + 1) if d == 0 else (slice(0, 1) if d < 0 else slice(edge + 1, edge + 2))
        shape = (edge if d == 0 else 1, edge, chans)
        for q in range(-1, per_slab + 1):
            total = jnp.zeros(shape, F32)
            for peer in range(nw):
                ids = idrecv[1 + d, peer]
                for j in range(live):
                    wide = jnp.concatenate([ids[j : j + 1]] * 2, axis=1)
                    hit = jnp.broadcast_to(wide.reshape(1, 1, chans), shape)
                    if d == 0:
                        value = crecv[peer, j].astype(F32)
                    else:
                        value = xedge[side(d), peer, j].astype(F32)[None]
                    total = total + jnp.where(hit == w * per_slab + q, value, 0.0)
            scale = lax.rsqrt(jnp.mean(total * total, axis=-1, keepdims=True) + 1e-05)
            normed = total * scale * gain_ref[...].reshape(1, 1, chans)
            begin = off + q * edge
            plane[where_x, begin : begin + edge, :] = normed

    for c in range(3):
        lhs2[:, :, c * chans : (c + 1) * chans] = plane[
            :, off + c - 1 : off + c - 1 + ydev, :
        ].astype(BF16)
    total = jnp.zeros((edge * ydev, chans), F32)
    for a in range(3):
        total = total + jnp.dot(
            lhs2[a : a + edge].reshape(edge * ydev, 3 * chans), w2[a], preferred_element_type=F32
        )
    residual = lhs2[1 : edge + 1, :, chans : 2 * chans].reshape(edge * ydev, chans).astype(F32)
    result = jnp.maximum(total * scale2_ref[...] + bias2_ref[...], 0.0) + residual
    out_ref[...] = result.reshape(edge, ydev, chans).astype(BF16)


def per_device(
    ng, nw,
    feats, brick_ids, conv3_w, conv3_scale, conv3_bias, bev_gain, conv2_w, conv2_scale, conv2_bias,
):
    slots, edge, chans = feats.shape[1], feats.shape[2], feats.shape[-1]
    live = slots - 1
    ydev = BY * edge // nw
    pad = edge + 2
    reach = edge // 2 + 2
    vmem = pl.BlockSpec(memory_space=pltpu.VMEM)
    hbm = pl.BlockSpec(memory_space=pl.ANY)
    dma = pltpu.SemaphoreType.DMA
    return pl.pallas_call(
        functools.partial(block_kernel, ng, nw, live),
        out_shape=jax.ShapeDtypeStruct((edge, ydev, chans), BF16),
        in_specs=[pl.BlockSpec(memory_space=pltpu.SMEM), hbm, hbm, hbm] + [vmem] * 5,
        out_specs=vmem,
        scratch_shapes=[
            pltpu.VMEM((live, edge, edge, edge, chans), BF16),
            pltpu.VMEM((live, pad, pad * edge, chans), F32),
            pltpu.VMEM((2, live, edge, edge, chans), BF16),
            pltpu.VMEM((2, live, edge, edge, chans), BF16),
            pltpu.VMEM((2, live, edge, edge, chans), BF16),
            pltpu.VMEM((2, 2, live, edge, chans), BF16),
            pltpu.VMEM((8, chans // 2), jnp.int32),
            pltpu.VMEM((3, nw, 8, chans // 2), jnp.int32),
            pltpu.VMEM((live, 2, pad, 16, chans), F32),
            pltpu.VMEM((live, reach, pad, 2 * edge, 3 * chans), BF16),
            pltpu.VMEM((9, 3 * chans, chans), BF16),
            pltpu.VMEM((3, 3 * chans, chans), BF16),
            pltpu.VMEM((live, edge, edge, chans), BF16),
            pltpu.VMEM((nw, live, edge, edge, chans), BF16),
            pltpu.VMEM((2, nw, live, edge, chans), BF16),
            pltpu.VMEM((pad, ydev + 2 * edge, chans), F32),
            pltpu.VMEM((pad, ydev, 3 * chans), BF16),
            dma((3,)),
            dma((3, nw)), dma((3, nw)),
            dma((2,)), dma((2,)),
            dma((2,)), dma((2,)),
            dma((2, 2)), dma((2, 2)),
            dma((3, nw)), dma((3, nw)),
        ],
        compiler_params=pltpu.CompilerParams(
            collective_id=0, has_side_effects=True, vmem_limit_bytes=56 << 20
        ),
    )(
        brick_ids,
        feats,
        conv3_w.reshape(9, 3 * chans, chans),
        conv2_w.reshape(3, 3 * chans, chans),
        conv3_scale.reshape(1, chans),
        conv3_bias.reshape(1, chans),
        bev_gain.reshape(1, chans),
        conv2_scale.reshape(1, chans),
        conv2_bias.reshape(1, chans),
    )


def solution(mesh):
    return jax.shard_map(
        functools.partial(per_device, mesh.shape["gx"], mesh.shape["wa"]),
        mesh=mesh,
        in_specs=(
            P("gx", "wa", None, None, None, None),
            P("gx", "wa"),
            P(),
            P(),
            P(),
            P(),
            P(),
            P(),
            P(),
        ),
        out_specs=P("gx", "wa", None),
        check_vma=False,
    )
```
